512 devices in a mesh: section: 4 (over x), sub: 32 (over z_lo, y), rng: 4 (over z_hi, core).
Axes of the slice: x: 4, y: 8, z: 8 (z_hi: 2, z_lo: 4; z = z_hi * 4 + z_lo), core: 2. Of those that a mesh axis runs over, the one named last changes fastest.
Arguments:
- echoes: bfloat16 [2, 32, 24, 16384], P(None, 'sub', 'section', 'rng'), may hold values from -6 to 6
- chirp: bfloat16 [2, 2048], replicated, may hold values from -0.25 to 0.25
- steer: bfloat16 [2, 32, 128, 24], P(None, 'sub'), may hold values from -2 to 2
- pulse_order: int32 [32, 24], P('sub'), may hold values from 0 to 23, each once within a row
- band_coef: bfloat16 [5, 32, 2, 2, 128, 16], P(None, 'sub'), may hold values from -2.5 to 2.5
- band_start: int32 [5, 32, 2, 128], P(None, 'sub'), may hold values from 0 to 112
- band_width: int32 [5, 32, 2, 128], P(None, 'sub'), may hold values from 1 to 16
Outputs:
- image: bfloat16 [2, 4096, 4, 4096], P(None, 'sub', 'rng', 'section')
The draws below stay inside these ranges and needn't reach their ends.
Inputs may be any that keep to these rules, and one draw needn't show every extreme that they name: `pulse_order`: each row is a permutation of the 24 aperture positions.
All inputs are finite; a program needn't handle non-finite values.
Results may differ from the reference program's by a relative error of at most 0.0085.
Values may be sent and summed in bfloat16 or wider, within the bound.
A program may use at most 64 MiB of HBM per device.

```python
import jax
import jax.numpy as jnp
from jax import lax

RS = 16384
K = 2048
BL = 128
BW = 16
LEVELS = 5
SUBS = 32
PSUB = 24
BEAMS = 4096
RC = 4096
N_SUB = 32
N_RNG = 4


def with_ends(entries, own_key, low, top_value):
    extent = entries.shape
    place = [jax.random.randint(jax.random.fold_in(own_key, axis), (), 0, extent[axis]) for axis in range(len(extent))]
    entries = entries.at[tuple(place)].set(low)
    longest = extent.index(max(extent))
    place[longest] = (place[longest] + 1) % extent[longest]
    return entries.at[tuple(place)].set(top_value)


def steps_of(own_key, extent, split, smallest, high):
    loudness, own = 1.0, jax.random.fold_in(own_key, 6)
    for dim, blocks in split:
        heights = jnp.exp(jax.random.uniform(jax.random.fold_in(own, dim), (blocks,), jnp.float32, smallest / len(split), high / len(split)))
        loudness = loudness * jnp.repeat(heights, extent[dim] // blocks).reshape([-1 if axis == dim else 1 for axis in range(len(extent))])
    return loudness


def centred(own_key, extent, scale, limit, pieces=(), held_as=jnp.bfloat16):
    entries = scale * jax.random.normal(own_key, extent, jnp.float32)
    if pieces:
        entries = entries * steps_of(own_key, extent, pieces, -0.22, 0.18)
    return jnp.clip(entries, -limit, limit).astype(held_as)


def setup_inputs(seed: int = 0) -> dict:
    seeds = jax.random.split(jax.random.key(seed), 8)
    echoes = centred(seeds[0], (2, SUBS, PSUB, RS), 1.0, 6.0, ((1, 32), (2, 4), (3, 4)))
    chirp = centred(seeds[1], (2, K), (1.0 / (2 * K) ** 0.5), 0.25)
    steer = centred(seeds[2], (2, SUBS, BL, PSUB), (1.0 / (2 * PSUB) ** 0.5), 2.0, ((1, 32),))
    pulse_order = jax.vmap(lambda own: jax.random.permutation(own, PSUB))(jax.random.split(seeds[3], SUBS)).reshape((SUBS, PSUB)).astype(jnp.int32)
    band_coef = centred(seeds[4], (LEVELS, SUBS, 2, 2, BL, BW), (1.0 / (2 * BW + 2) ** 0.5), 2.5, ((1, 32),))
    band_start = with_ends(jax.random.randint(seeds[5], (LEVELS, SUBS, 2, BL), 0, BL - BW + 1), jax.random.fold_in(seeds[5], 1), 0, BL - BW).astype(jnp.int32)
    band_width = with_ends(jax.random.randint(seeds[6], (LEVELS, SUBS, 2, BL), 1, BW + 1), jax.random.fold_in(seeds[6], 1), 1, BW).astype(jnp.int32)
    return {"echoes": echoes, "chirp": chirp, "steer": steer, "pulse_order": pulse_order, "band_coef": band_coef, "band_start": band_start, "band_width": band_width}


def compress_and_form(inputs):
    signal, weights_all, order_row, kernel_parts = inputs
    length = 1 << (RS + K - 1).bit_length()
    wave = lax.complex(signal[0].astype(jnp.float32), signal[1].astype(jnp.float32))
    kernel = lax.complex(kernel_parts[0].astype(jnp.float32), kernel_parts[1].astype(jnp.float32))
    spectrum = jnp.fft.fft(wave, n=length, axis=1) * jnp.conj(jnp.fft.fft(kernel, n=length))[None, :]
    result = jnp.fft.ifft(spectrum, axis=1)[:, :RS]
    compressed = jnp.stack([jnp.real(result), jnp.imag(result)]).astype(jnp.bfloat16)
    weights = jnp.take(weights_all, order_row, axis=2)
    real_part = jnp.dot(weights[0], compressed[0], preferred_element_type=jnp.float32) - jnp.dot(weights[1], compressed[1], preferred_element_type=jnp.float32)
    imag_part = jnp.dot(weights[0], compressed[1], preferred_element_type=jnp.float32) + jnp.dot(weights[1], compressed[0], preferred_element_type=jnp.float32)
    return jnp.stack([real_part, imag_part]).astype(jnp.bfloat16)


def reference(echoes, chirp, steer, pulse_order, band_coef, band_start, band_width):
    kernels = jnp.broadcast_to(chirp[None], (N_SUB, 2, K))
    images = lax.map(compress_and_form, (jnp.transpose(echoes, (1, 0, 2, 3)), jnp.transpose(steer, (1, 0, 2, 3)), pulse_order, kernels))
    nbits = N_SUB.bit_length() - 1
    for level in range(LEVELS):
        flip = 1 << (level % nbits)

        def merge_one(inputs):
            position, coef_sub, start_sub, width_sub = inputs
            own = images[position].astype(jnp.float32)
            other = images[jnp.bitwise_xor(position, flip)].astype(jnp.float32)
            total_real = jnp.zeros((BL, RS), jnp.float32)
            total_imag = jnp.zeros((BL, RS), jnp.float32)
            for side in range(2):
                source = own if side == 0 else other
                for tap in range(BW):
                    picked_rows = (start_sub[side] + tap).astype(jnp.int32)
                    gathered = source[:, picked_rows, :]
                    active = (tap < width_sub[side]).astype(jnp.float32)
                    weight_real = (coef_sub[side, 0, :, tap].astype(jnp.float32) * active)[:, None]
                    weight_imag = (coef_sub[side, 1, :, tap].astype(jnp.float32) * active)[:, None]
                    total_real = total_real + weight_real * gathered[0] - weight_imag * gathered[1]
                    total_imag = total_imag + weight_real * gathered[1] + weight_imag * gathered[0]
            return jnp.stack([total_real, total_imag]).astype(jnp.bfloat16)

        images = lax.map(merge_one, (jnp.arange(N_SUB, dtype=jnp.int32), band_coef[level], band_start[level], band_width[level]))
    image = jnp.transpose(images, (1, 0, 2, 3)).reshape(2, BEAMS, N_RNG, RC)
    return image
```

```python
import functools

import jax
import jax.numpy as jnp
from jax import lax
from jax.experimental import pallas as pl
from jax.experimental.pallas import tpu as pltpu
from jax.sharding import PartitionSpec as P

F32 = jnp.float32
BF16 = jnp.bfloat16
MESH = pl.DeviceIdType.MESH

NX = 4
NY = 8
NZ = 4
NG = 4
PP = 6
PS = 24
RC = 4096
TAPS = 2048
CB = 128
QB = 128
SEC = 1024
NCH = 4
CW = SEC // NCH
BLK = 4 * PS
GROUPS = ((0, 1), (2, 3))


def dot(a, b):
    return jnp.dot(a, b, preferred_element_type=F32)


def dot_nt(a, b):
    return lax.dot_general(a, b, (((1,), (1,)), ((), ())), preferred_element_type=F32)


def flip(v, bit):
    return v + bit - 2 * bit * ((v // bit) % 2)


def one_hot(shape, dim0_of_dim1):
    rows = lax.broadcasted_iota(jnp.int32, shape, 0)
    cols = lax.broadcasted_iota(jnp.int32, shape, 1)
    return jnp.where(rows == dim0_of_dim1(cols), 1.0, 0.0).astype(BF16)


def kernel(
    echo, chirp, steer, order, coef, start, width, out,
    halo, xf, x2, table, comp, recv, gath, pmat, zcoef, zstart, mats,
    tx0, tx1, tx2, tx3, ts, tt, tmat, own, psend, precv, ostage,
    s_rim, r_rim, s_par, r_par, s_t, r_t, s_a, r_a, s_g, r_g, s_p, r_p, s_o,
):
    sec = lax.axis_index("section")
    sub = lax.axis_index("sub")
    rng = lax.axis_index("rng")
    y = sub % NY
    z = sub // NY
    base = z * NY

    def at_y(v):
        return {"sub": base + v}

    def at_z(v):
        return {"sub": v * NY + y}

    z1 = flip(z, 1)
    z2 = flip(z, 2)
    z3 = flip(z2, 1)
    y1 = flip(y, 1)
    y2 = flip(y, 2)
    y4 = flip(y, 4)
    up = (y + 1) % NY
    down = (y + NY - 1) % NY

    barrier = pltpu.get_barrier_semaphore()
    peers = [{"rng": (rng + 1) % NG}, {"rng": (rng + NG - 1) % NG}]
    for d in range(1, NX):
        other = (sec + d) % NX
        peers.append({"section": other})
        peers.append({"section": other, "sub": z2 * NY + y})
    peers += [at_z(z1), at_z(z2), at_z(z3), at_y(up), at_y(down), at_y(flip(y, 2)), at_y(y4)]
    for peer in peers:
        pl.semaphore_signal(barrier, inc=1, device_id=peer, device_id_type=MESH)
    pl.semaphore_wait(barrier, len(peers))

    def send(src, dst, ssem, rsem, to):
        return pltpu.make_async_remote_copy(
            src_ref=src, dst_ref=dst, send_sem=ssem, recv_sem=rsem,
            device_id=to, device_id_type=MESH,
        )

    rim = send(echo.at[:, :, 0:TAPS], halo, s_rim, r_rim, {"rng": (rng + NG - 1) % NG})
    rim.start()

    select = one_hot((PS, PS), lambda cols: order[...])
    eye32 = one_hot((32, PS), lambda cols: cols)
    sel_t = dot_nt(eye32, select).astype(BF16)
    ts[0:32, 0:QB] = dot(sel_t, steer[0]).astype(BF16)
    ts[0:32, QB:] = dot(sel_t, steer[1]).astype(BF16)
    t0 = send(ts.at[0:32], tx0, s_t.at[0], r_t.at[0], at_y(y1))
    t0.start()

    taps = lax.broadcasted_iota(jnp.int32, (16, QB), 0)
    for level in range(5):
        for side in range(2):
            keep = taps < width[level, side : side + 1, :]
            for part in range(2):
                i = level * 4 + side * 2 + part
                entry = jnp.where(keep, coef[i].astype(F32), 0.0)
                pmat[i] = entry.astype(BF16)
                if level >= 3:
                    zcoef[0, i - 12] = entry.astype(BF16)
            if level >= 3:
                zstart[0, (level - 3) * 2 + side : (level - 3) * 2 + side + 1, :] = start[level, side : side + 1, :]
    zstart[0, 4:8, :] = jnp.zeros((4, QB), jnp.int32)
    par = []
    for d, to in ((1, z1), (2, z2), (3, z3)):
        par.append(send(zcoef.at[0], zcoef.at[d], s_par.at[0, d], r_par.at[0, d], at_z(to)))
        par.append(send(zstart.at[0], zstart.at[d], s_par.at[1, d], r_par.at[1, d], at_z(to)))
    for copy in par:
        copy.start()

    def band(slot, real, imag, first):
        offset = lax.broadcasted_iota(jnp.int32, (QB, QB), 0) - first
        re = jnp.zeros((QB, QB), F32)
        im = jnp.zeros((QB, QB), F32)
        for t in range(16):
            hit = offset == t
            re = jnp.where(hit, real[t : t + 1, :], re)
            im = jnp.where(hit, imag[t : t + 1, :], im)
        re_b = re.astype(BF16)
        mats[slot, 0:QB, 0:QB] = re_b
        mats[slot, QB:, QB:] = re_b
        mats[slot, 0:QB, QB:] = im.astype(BF16)
        mats[slot, QB:, 0:QB] = (-im).astype(BF16)

    def own_band(level, side):
        i = level * 4 + side * 2
        band(level * 2 + side, pmat[i].astype(F32), pmat[i + 1].astype(F32), start[level, side : side + 1, :])

    def far_band(slot, d, row):
        band(slot, zcoef[d, row * 2].astype(F32), zcoef[d, row * 2 + 1].astype(F32), zstart[d, row : row + 1, :])

    wide = TAPS + 2 * CB
    for part in range(2):
        line = jnp.concatenate([chirp[part : part + 1, :].astype(F32), jnp.zeros((1, 2 * CB), F32)], axis=1)
        line = jnp.broadcast_to(line, (CB, wide))
        table[part * CB : (part + 1) * CB, :] = pltpu.roll(line, 0, 1, stride=1, stride_axis=0).astype(BF16)

    def load_rows(ref, blocks, first):
        lanes = blocks * CB
        for part in range(2):
            for p in range(PP):
                xf[part * 8 + p : part * 8 + p + 1, 0:lanes] = ref[p, part : part + 1, :].astype(F32)
            xf[part * 8 + PP : part * 8 + 8, 0:lanes] = jnp.zeros((8 - PP, lanes), F32)
        for b in range(blocks):
            tile = xf[:, b * CB : (b + 1) * CB]
            if ref is halo:
                tile = jnp.where(rng == NG - 1, jnp.zeros_like(tile), tile)
            tile = tile.astype(BF16)
            x2[first + b, :, 0:CB] = tile
            if first + b > 0:
                x2[first + b - 1, :, CB:] = tile

    nb = RC // CB
    nh = TAPS // CB

    def compress(first):
        rows = 16
        total = None
        for j in range(wide // (2 * CB)):
            lhs = x2[first + 2 * j : first + 2 * j + rows].reshape(rows * 16, 2 * CB)
            piece = dot_nt(lhs, table[:, 2 * j * CB : 2 * (j + 1) * CB])
            total = piece if total is None else total + piece
        for b in range(rows):
            re_rows = total[b * 16 : b * 16 + 8]
            im_rows = total[b * 16 + 8 : b * 16 + 16]
            re = re_rows[:, 0:CB] + im_rows[:, CB:]
            im = im_rows[:, 0:CB] - re_rows[:, CB:]
            at = (first + b) * CB
            comp[:, at : at + CB] = jnp.concatenate([re, im], axis=0).astype(BF16)

    def scatter(s):
        lanes = comp.at[:, s * SEC : (s + 1) * SEC]
        near = send(lanes, recv.at[0, sec], s_a.at[0, s], r_a.at[0, sec], {"section": s})
        far = send(lanes, recv.at[1, sec], s_a.at[1, s], r_a.at[1, sec], {"section": s, "sub": z2 * NY + y})
        far.start()

        @pl.when(sec != s)
        def _():
            near.start()

        return near, far

    load_rows(echo, nb, 0)
    compress(0)
    sent = [scatter(0), scatter(1)]
    rim.wait()
    load_rows(halo, nh, nb)
    x2[nb + nh - 1, :, CB:] = jnp.zeros((16, CB), BF16)
    compress(16)
    sent += [scatter(2), scatter(3)]
    recv[0, sec] = comp[:, pl.ds(pl.multiple_of(sec * SEC, SEC), SEC)]

    def grow(level, mine, theirs, rows):
        at_low = (y // (1 << level)) % 2 == 0
        a = dot(mine, mats[level * 2])[0:rows]
        b = dot(theirs, mats[level * 2 + 1])[0:rows]
        low = jnp.where(at_low, a, b)
        high = jnp.where(at_low, b, a)
        return jnp.concatenate([low, high], axis=0).astype(BF16)

    own_band(0, 0)
    own_band(0, 1)
    t0.wait()
    ts[32:80] = grow(0, ts[0:32], tx0[...], PS)
    t1 = send(ts.at[32:80], tx1, s_t.at[1], r_t.at[1], at_y(y2))
    t1.start()

    for x in range(NX):
        for zz in range(2):
            arrival = send(comp.at[:, 0:SEC], recv.at[zz, x], s_a.at[zz, 0], r_a.at[zz, x], {"section": sec})
            if zz == 0:
                @pl.when(sec != x)
                def _():
                    arrival.wait_recv()
            else:
                arrival.wait_recv()
    rows_i = lax.broadcasted_iota(jnp.int32, (BLK, 128), 0)
    cols_i = lax.broadcasted_iota(jnp.int32, (BLK, 128), 1)
    hot = jnp.zeros((BLK, 128), F32)
    for zz in range(2):
        for part in range(2):
            for x in range(NX):
                r0 = zz * 2 * PS + part * PS + x * PP
                c0 = zz * 64 + x * 16 + part * 8
                inside = (rows_i >= r0) & (rows_i < r0 + PP) & (cols_i - rows_i == c0 - r0)
                hot = jnp.where(inside, 1.0, hot)
    hot = hot.astype(BF16)
    for c in range(NCH):
        rows = recv[:, :, :, c * CW : (c + 1) * CW].reshape(2 * NX * 16, CW)
        gath[c, y] = dot(hot, rows).astype(BF16)

    def hop(direction, c, s):
        if direction == 0:
            at = (y + NY - s) % NY
            to = up
        else:
            at = (y + s) % NY
            to = down
        return send(gath.at[c, at], gath.at[c, at], s_g.at[direction, c, s], r_g.at[direction, c, s], at_y(to))

    def arrived(direction, c, s):
        if direction == 0:
            at = (y + 2 * NY - 1 - s) % NY
        else:
            at = (y + 1 + s) % NY
        return send(gath.at[c, at], gath.at[c, at], s_g.at[direction, c, s], r_g.at[direction, c, s], at_y(up))

    def legs(c, s):
        return (0, 1) if s < 3 else (c % 2,)

    def ring(group, s):
        for c in GROUPS[group]:
            for direction in legs(c, s):
                if s > 0:
                    arrived(direction, c, s - 1).wait_recv()
                hop(direction, c, s).start()

    def settle(group):
        for c in GROUPS[group]:
            for direction in (0, 1):
                last = 3 if direction in legs(c, 3) else 2
                if last == 3:
                    arrived(direction, c, 3).wait_recv()
                else:
                    arrived(direction, c, 2).wait_recv()

    ring(0, 0)
    ring(1, 0)
    own_band(1, 0)
    own_band(1, 1)
    t1.wait()
    ts[80:176] = grow(1, ts[32:80], tx1[...], 2 * PS)
    t2 = send(ts.at[80:176], tx2, s_t.at[2], r_t.at[2], at_y(y4))
    t2.start()
    ring(0, 1)
    own_band(2, 0)
    own_band(2, 1)
    ring(1, 1)
    t2.wait()
    ts[176:368] = grow(2, ts[80:176], tx2[...], 4 * PS)
    t3 = send(ts.at[176:368], tx3, s_t.at[3], r_t.at[3], at_z(z2))
    t3.start()
    ring(0, 2)
    for level in (3, 4):
        for side in range(2):
            own_band(level, side)
    for copy in par:
        copy.wait()
    far_band(10, 1, 1)
    far_band(11, 1, 2)
    far_band(12, 1, 3)
    ring(1, 2)
    far_band(13, 2, 0)
    far_band(14, 3, 1)
    ring(0, 3)

    def chain(rows, first, second):
        return dot(dot(rows, mats[first]).astype(BF16), mats[second]).reshape(NY, PS, 2 * QB)

    def turned(rows):
        return jnp.concatenate([-rows[:, :, QB:], rows[:, :, 0:QB]], axis=2)

    eye = one_hot((2 * QB, 2 * QB), lambda cols: cols)
    near_rows = ts[176:368]
    a0 = chain(near_rows, 6, 8)
    b0 = chain(near_rows, 10, 11)
    t3.wait()
    far_rows = tx3[...]
    a1 = chain(far_rows, 13, 9)
    b1 = chain(far_rows, 14, 12)
    for i, (near_t, far_t) in enumerate(((a0, a1), (b0, b1))):
        full = jnp.concatenate([near_t, turned(near_t), far_t, turned(far_t)], axis=1)
        tt[...] = full.reshape(NY * BLK, 2 * QB).astype(BF16)
        tmat[i * 2 * QB : (i + 1) * 2 * QB, :] = dot_nt(eye, tt[...]).astype(BF16)
    ring(1, 3)

    swaps = []
    for group in range(2):
        settle(group)
        for c in GROUPS[group]:
            pulses = gath[c].reshape(NY * BLK, CW)
            psend[c] = dot(tmat[2 * QB :, :], pulses).astype(BF16)
            swap = send(psend.at[c], precv.at[c], s_p.at[c], r_p.at[c], at_z(z1))
            swap.start()
            swaps.append(swap)
            own[c] = dot(tmat[0 : 2 * QB, :], pulses)
    stores = []
    for c in range(NCH):
        swaps[c].wait()
        total = own[c] + precv[c].astype(F32)
        ostage[c] = total.reshape(2, QB, CW).astype(BF16)
        store = pltpu.make_async_copy(ostage.at[c], out.at[:, :, c * CW : (c + 1) * CW], s_o.at[c])
        store.start()
        stores.append(store)
    for store in stores:
        store.wait()
    for s, (near, far) in enumerate(sent):
        far.wait_send()

        @pl.when(sec != s)
        def _():
            near.wait_send()

    for c in range(NCH):
        for s in range(4):
            for direction in legs(c, s):
                hop(direction, c, s).wait_send()


def on_device(echoes, chirp, steer, pulse_order, band_coef, band_start, band_width):
    echo = jnp.transpose(echoes[:, 0], (1, 0, 2))
    steer_t = jnp.swapaxes(steer[:, 0], 1, 2)
    coef = jnp.swapaxes(band_coef[:, 0], 3, 4).reshape(20, 16, QB)
    dma = pltpu.SemaphoreType.DMA
    vmem = pltpu.VMEM
    image = pl.pallas_call(
        kernel,
        out_shape=jax.ShapeDtypeStruct((2, QB, SEC), BF16),
        in_specs=[pl.BlockSpec(memory_space=pltpu.VMEM)] * 7,
        out_specs=pl.BlockSpec(memory_space=pl.ANY),
        scratch_shapes=[
            vmem((PP, 2, TAPS), BF16),
            vmem((16, RC), F32),
            vmem((48, 16, 2 * CB), BF16),
            vmem((2 * CB, TAPS + 2 * CB), BF16),
            vmem((16, RC), BF16),
            vmem((2, NX, 16, SEC), BF16),
            vmem((NCH, NY, BLK, CW), BF16),
            vmem((20, 16, QB), BF16),
            vmem((4, 8, 16, QB), BF16),
            vmem((4, 8, QB), jnp.int32),
            vmem((15, 2 * QB, 2 * QB), BF16),
            vmem((32, 2 * QB), BF16),
            vmem((2 * PS, 2 * QB), BF16),
            vmem((4 * PS, 2 * QB), BF16),
            vmem((8 * PS, 2 * QB), BF16),
            vmem((368, 2 * QB), BF16),
            vmem((NY * BLK, 2 * QB), BF16),
            vmem((4 * QB, NY * BLK), BF16),
            vmem((NCH, 2 * QB, CW), F32),
            vmem((NCH, 2 * QB, CW), BF16),
            vmem((NCH, 2 * QB, CW), BF16),
            vmem((NCH, 2, QB, CW), BF16),
            dma, dma,
            dma((2, 4)), dma((2, 4)),
            dma((4,)), dma((4,)),
            dma((2, NX)), dma((2, NX)),
            dma((2, NCH, 4)), dma((2, NCH, 4)),
            dma((NCH,)), dma((NCH,)),
            dma((NCH,)),
        ],
        compiler_params=pltpu.CompilerParams(
            collective_id=0, has_side_effects=True, vmem_limit_bytes=40 << 20
        ),
        name="aperture",
    )(echo, chirp, steer_t, pulse_order, coef, band_start[:, 0], band_width[:, 0])
    return image[:, :, None, :]


def solution(mesh):
    return jax.shard_map(
        on_device,
        mesh=mesh,
        in_specs=(
            P(None, "sub", "section", "rng"),
            P(),
            P(None, "sub", None, None),
            P("sub", None),
            P(None, "sub", None, None, None, None),
            P(None, "sub", None, None),
            P(None, "sub", None, None),
        ),
        out_specs=P(None, "sub", "rng", "section"),
        check_vma=False,
    )
```

```python
import functools

import jax
import jax.numpy as jnp
from jax import lax
from jax.experimental import pallas as pl
from jax.experimental.pallas import tpu as pltpu
from jax.sharding import PartitionSpec as P

F32 = jnp.float32
BF16 = jnp.bfloat16
MESH = pl.DeviceIdType.MESH

NX = 4
NY = 8
NZ = 4
NG = 4
PP = 6
PS = 24
RC = 4096
TAPS = 2048
CB = 128
QB = 128
SEC = 1024
NCH = 4
CW = SEC // NCH
BLK = 4 * PS


def staggered(chunks, lag):
    steps = [(2 * s + lag * c, c, s) for c in range(chunks) for s in range(5)]
    return [(c, s) for _, c, s in sorted(steps)]


ORDER = staggered(NCH, 1.5)


def dot(a, b):
    return jnp.dot(a, b, preferred_element_type=F32)


def dot_nt(a, b):
    return lax.dot_general(a, b, (((1,), (1,)), ((), ())), preferred_element_type=F32)


def flip(v, bit):
    return v + bit - 2 * bit * ((v // bit) % 2)


def one_hot(shape, dim0_of_dim1):
    rows = lax.broadcasted_iota(jnp.int32, shape, 0)
    cols = lax.broadcasted_iota(jnp.int32, shape, 1)
    return jnp.where(rows == dim0_of_dim1(cols), 1.0, 0.0).astype(BF16)


def kernel(
    echo_h, chirp_h, steer_h, order_h, coef_h, start_h, width_h, out,
    echo, chirp, steer, order, coef, start, width,
    halo, xf, x2, table, comp, recv, gath, pmat, zcoef, zstart, mats,
    tx0, tx1, tx2, tx3, ts, tt, tmat, psend, own, got,
    s_in, s_rim, r_rim, s_par, r_par, s_t, r_t, s_a, r_a, s_g, r_g, s_p, r_p,
):
    loads = []
    pairs = ((steer_h, steer), (order_h, order), (chirp_h, chirp), (coef_h, coef),
             (start_h, start), (width_h, width), (echo_h, echo))
    for i, (src, dst) in enumerate(pairs):
        loads.append(pltpu.make_async_copy(src, dst, s_in.at[i]))
        loads[-1].start()

    sec = lax.axis_index("section")
    sub = lax.axis_index("sub")
    rng = lax.axis_index("rng")
    y = sub % NY
    z = sub // NY
    base = z * NY

    def at_y(v):
        return {"sub": base + v}

    def at_z(v):
        return {"sub": v * NY + y}

    z1 = flip(z, 1)
    z2 = flip(z, 2)
    z3 = flip(z2, 1)
    y1 = flip(y, 1)
    y2 = flip(y, 2)
    y4 = flip(y, 4)
    up = (y + 1) % NY
    down = (y + NY - 1) % NY

    barrier = pltpu.get_barrier_semaphore()
    peers = [{"rng": (rng + 1) % NG}, {"rng": (rng + NG - 1) % NG}]
    for d in range(1, NX):
        other = (sec + d) % NX
        peers.append({"section": other})
        peers.append({"section": other, "sub": z2 * NY + y})
    peers += [at_z(z1), at_z(z2), at_z(z3), at_y(up), at_y(down), at_y(flip(y, 2)), at_y(y4)]
    for peer in peers:
        pl.semaphore_signal(barrier, inc=1, device_id=peer, device_id_type=MESH)
    for i in range(2):
        loads[i].wait()
    select = one_hot((PS, PS), lambda cols: order[...])
    eye32 = one_hot((32, PS), lambda cols: cols)
    sel_t = dot_nt(eye32, select).astype(BF16)
    ts[0:32, 0:QB] = dot(sel_t, steer[0]).astype(BF16)
    ts[0:32, QB:] = dot(sel_t, steer[1]).astype(BF16)

    loads[2].wait()
    wide = TAPS + 2 * CB
    for part in range(2):
        line = jnp.concatenate([chirp[part : part + 1, :].astype(F32), jnp.zeros((1, 2 * CB), F32)], axis=1)
        line = jnp.broadcast_to(line, (CB, wide))
        table[part * CB : (part + 1) * CB, :] = pltpu.roll(line, 0, 1, stride=1, stride_axis=0).astype(BF16)

    def load_rows(ref, blocks, first):
        lanes = blocks * CB
        for part in range(2):
            for p in range(PP):
                xf[part * 8 + p : part * 8 + p + 1, 0:lanes] = ref[p, part : part + 1, :].astype(F32)
            xf[part * 8 + PP : part * 8 + 8, 0:lanes] = jnp.zeros((8 - PP, lanes), F32)
        for b in range(blocks):
            tile = xf[:, b * CB : (b + 1) * CB]
            if ref is halo:
                tile = jnp.where(rng == NG - 1, jnp.zeros_like(tile), tile)
            tile = tile.astype(BF16)
            x2[first + b, :, 0:CB] = tile
            if first + b > 0:
                x2[first + b - 1, :, CB:] = tile

    nb = RC // CB
    nh = TAPS // CB

    def compress(first):
        rows = 16
        total = None
        for j in range(wide // (2 * CB)):
            lhs = x2[first + 2 * j : first + 2 * j + rows].reshape(rows * 16, 2 * CB)
            piece = dot_nt(lhs, table[:, 2 * j * CB : 2 * (j + 1) * CB])
            total = piece if total is None else total + piece
        for b in range(rows):
            re_rows = total[b * 16 : b * 16 + 8]
            im_rows = total[b * 16 + 8 : b * 16 + 16]
            re = re_rows[:, 0:CB] + im_rows[:, CB:]
            im = im_rows[:, 0:CB] - re_rows[:, CB:]
            at = (first + b) * CB
            comp[:, at : at + CB] = jnp.concatenate([re, im], axis=0).astype(BF16)

    loads[6].wait()
    load_rows(echo, nb, 0)
    compress(0)

    pl.semaphore_wait(barrier, len(peers))

    def send(src, dst, ssem, rsem, to):
        return pltpu.make_async_remote_copy(
            src_ref=src, dst_ref=dst, send_sem=ssem, recv_sem=rsem,
            device_id=to, device_id_type=MESH,
        )

    rim = send(echo_h.at[:, :, 0:TAPS], halo, s_rim, r_rim, {"rng": (rng + NG - 1) % NG})

    @pl.when(rng > 0)
    def _():
        rim.start()

    t0 = send(ts.at[0:32], tx0, s_t.at[0], r_t.at[0], at_y(y1))
    t0.start()

    def scatter(s):
        lanes = comp.at[:, s * SEC : (s + 1) * SEC]
        near = send(lanes, recv.at[0, sec], s_a.at[0, s], r_a.at[0, sec], {"section": s})
        far = send(lanes, recv.at[1, sec], s_a.at[1, s], r_a.at[1, sec], {"section": s, "sub": z2 * NY + y})
        far.start()

        @pl.when(sec != s)
        def _():
            near.start()

        return near, far

    sent = [scatter(0), scatter(1)]

    for i in range(3, 6):
        loads[i].wait()
    taps = lax.broadcasted_iota(jnp.int32, (16, QB), 0)
    for level in range(5):
        for side in range(2):
            keep = taps < width[level, side : side + 1, :]
            for part in range(2):
                i = level * 4 + side * 2 + part
                entry = jnp.where(keep, coef[i].astype(F32), 0.0)
                pmat[i] = entry.astype(BF16)
                if level >= 3:
                    zcoef[0, i - 12] = entry.astype(BF16)
            if level >= 3:
                zstart[0, (level - 3) * 2 + side : (level - 3) * 2 + side + 1, :] = start[level, side : side + 1, :]
    zstart[0, 4:8, :] = jnp.zeros((4, QB), jnp.int32)
    par = []
    for d, to, lo, hi in ((1, z1, 2, 8), (2, z2, 0, 2), (3, z3, 2, 4)):
        par.append(send(zcoef.at[0, lo:hi], zcoef.at[d, lo:hi], s_par.at[0, d], r_par.at[0, d], at_z(to)))
        par.append(send(zstart.at[0], zstart.at[d], s_par.at[1, d], r_par.at[1, d], at_z(to)))

    def band(slot, real, imag, first):
        offset = lax.broadcasted_iota(jnp.int32, (QB, QB), 0) - first
        re = jnp.zeros((QB, QB), F32)
        im = jnp.zeros((QB, QB), F32)
        for t in range(16):
            hit = offset == t
            re = jnp.where(hit, real[t : t + 1, :], re)
            im = jnp.where(hit, imag[t : t + 1, :], im)
        re_b = re.astype(BF16)
        mats[slot, 0:QB, 0:QB] = re_b
        mats[slot, QB:, QB:] = re_b
        mats[slot, 0:QB, QB:] = im.astype(BF16)
        mats[slot, QB:, 0:QB] = (-im).astype(BF16)

    def own_band(level, side):
        i = level * 4 + side * 2
        band(level * 2 + side, pmat[i].astype(F32), pmat[i + 1].astype(F32), start[level, side : side + 1, :])

    def far_band(slot, d, row):
        band(slot, zcoef[d, row * 2].astype(F32), zcoef[d, row * 2 + 1].astype(F32), zstart[d, row : row + 1, :])

    def grow(level, mine, theirs, rows):
        at_low = (y // (1 << level)) % 2 == 0
        a = dot(mine, mats[level * 2])[0:rows]
        b = dot(theirs, mats[level * 2 + 1])[0:rows]
        low = jnp.where(at_low, a, b)
        high = jnp.where(at_low, b, a)
        return jnp.concatenate([low, high], axis=0).astype(BF16)

    own_band(0, 0)
    own_band(0, 1)
    t0.wait()
    ts[32:80] = grow(0, ts[0:32], tx0[...], PS)
    t1 = send(ts.at[32:80], tx1, s_t.at[1], r_t.at[1], at_y(y2))
    t1.start()

    @pl.when(rng < NG - 1)
    def _():
        rim.wait_recv()

    load_rows(halo, nh, nb)
    x2[nb + nh - 1, :, CB:] = jnp.zeros((16, CB), BF16)
    compress(16)
    sent += [scatter(2), scatter(3)]
    recv[0, sec] = comp[:, pl.ds(pl.multiple_of(sec * SEC, SEC), SEC)]
    rows_i = lax.broadcasted_iota(jnp.int32, (BLK, 128), 0)
    cols_i = lax.broadcasted_iota(jnp.int32, (BLK, 128), 1)
    hot = jnp.zeros((BLK, 128), F32)
    for zz in range(2):
        for part in range(2):
            for x in range(NX):
                r0 = zz * 2 * PS + part * PS + x * PP
                c0 = zz * 64 + x * 16 + part * 8
                inside = (rows_i >= r0) & (rows_i < r0 + PP) & (cols_i - rows_i == c0 - r0)
                hot = jnp.where(inside, 1.0, hot)
    hot = hot.astype(BF16)
    own_band(1, 0)
    own_band(1, 1)
    t1.wait()
    ts[80:176] = grow(1, ts[32:80], tx1[...], 2 * PS)
    t2 = send(ts.at[80:176], tx2, s_t.at[2], r_t.at[2], at_y(y4))
    t2.start()

    for x in range(NX):
        for zz in range(2):
            arrival = send(comp.at[:, 0:SEC], recv.at[zz, x], s_a.at[zz, 0], r_a.at[zz, x], {"section": sec})
            if zz == 0:
                @pl.when(sec != x)
                def _():
                    arrival.wait_recv()
            else:
                arrival.wait_recv()
    for c in range(NCH):
        rows = recv[:, :, :, c * CW : (c + 1) * CW].reshape(2 * NX * 16, CW)
        gath[c, y] = dot(hot, rows).astype(BF16)

    def hop(direction, c, s):
        if direction == 0:
            at = (y + NY - s) % NY
            to = up
        else:
            at = (y + s) % NY
            to = down
        return send(gath.at[c, at], gath.at[c, at], s_g.at[direction, c, s], r_g.at[direction, c, s], at_y(to))

    def arrived(direction, c, s):
        if direction == 0:
            at = (y + 2 * NY - 1 - s) % NY
        else:
            at = (y + 1 + s) % NY
        return send(gath.at[c, at], gath.at[c, at], s_g.at[direction, c, s], r_g.at[direction, c, s], at_y(up))

    def legs(c, s):
        return (0, 1) if s < 3 else (c % 2,)

    def ring(c, s):
        for direction in legs(c, s):
            if s > 0:
                arrived(direction, c, s - 1).wait_recv()
            hop(direction, c, s).start()

    def settle(c):
        for direction in (0, 1):
            arrived(direction, c, 3 if direction in legs(c, 3) else 2).wait_recv()

    state = {}

    def part_a():
        for copy in par:
            copy.start()
        own_band(2, 0)
        own_band(2, 1)
        t2.wait()
        ts[176:368] = grow(2, ts[80:176], tx2[...], 4 * PS)
        state["t3"] = send(ts.at[176:368], tx3, s_t.at[3], r_t.at[3], at_z(z2))
        state["t3"].start()

    def part_b():
        for level in (3, 4):
            for side in range(2):
                own_band(level, side)

    def part_c():
        for copy in par:
            copy.wait()
        far_band(10, 1, 1)
        far_band(11, 1, 2)
        far_band(12, 1, 3)
        far_band(13, 2, 0)
        far_band(14, 3, 1)

    def chain(rows, first, second):
        return dot(dot(rows, mats[first]).astype(BF16), mats[second]).reshape(NY, PS, 2 * QB)

    def turned(rows):
        return jnp.concatenate([-rows[:, :, QB:], rows[:, :, 0:QB]], axis=2)

    eye = one_hot((2 * QB, 2 * QB), lambda cols: cols)

    def part_d():
        near_rows = ts[176:368]
        a0 = chain(near_rows, 6, 8)
        b0 = chain(near_rows, 10, 11)
        state["t3"].wait()
        far_rows = tx3[...]
        a1 = chain(far_rows, 13, 9)
        b1 = chain(far_rows, 14, 12)
        for i, (near_t, far_t) in enumerate(((a0, a1), (b0, b1))):
            full = jnp.concatenate([near_t, turned(near_t), far_t, turned(far_t)], axis=1)
            tt[...] = full.reshape(NY * BLK, 2 * QB).astype(BF16)
            tmat[i * 2 * QB : (i + 1) * 2 * QB, :] = dot_nt(eye, tt[...]).astype(BF16)

    swaps = []

    def image(c):
        settle(c)
        pulses = gath[c].reshape(NY * BLK, CW)
        psend[c] = dot(tmat[2 * QB :, :], pulses).reshape(2, QB, CW).astype(BF16)
        swap = send(psend.at[c], got.at[c], s_p.at[c], r_p.at[c], at_z(z1))
        swap.start()
        swaps.append(swap)
        own[c] = dot(tmat[0 : 2 * QB, :], pulses).reshape(2, QB, CW)

    parts = {NCH: part_a, NCH + NCH // 2: part_b, 2 * NCH: part_c, 2 * NCH + NCH // 2: part_d}
    for i, (c, s) in enumerate(ORDER):
        if s == 4:
            image(c)
        else:
            ring(c, s)
        if i + 1 in parts:
            parts[i + 1]()
    for (c, _), swap in zip([step for step in ORDER if step[1] == 4], swaps):
        swap.wait()
        out[:, :, c * CW : (c + 1) * CW] = (own[c] + got[c].astype(F32)).astype(BF16)
    for s, (near, far) in enumerate(sent):
        far.wait_send()

        @pl.when(sec != s)
        def _():
            near.wait_send()

    @pl.when(rng > 0)
    def _():
        rim.wait_send()

    for c in range(NCH):
        for s in range(4):
            for direction in legs(c, s):
                hop(direction, c, s).wait_send()


def on_device(echoes, chirp, steer, pulse_order, band_coef, band_start, band_width):
    echo = jnp.transpose(echoes[:, 0], (1, 0, 2))
    steer_t = jnp.swapaxes(steer[:, 0], 1, 2)
    coef = jnp.swapaxes(band_coef[:, 0], 3, 4).reshape(20, 16, QB)
    args = (echo, chirp, steer_t, pulse_order, coef, band_start[:, 0], band_width[:, 0])
    dma = pltpu.SemaphoreType.DMA
    vmem = pltpu.VMEM
    image = pl.pallas_call(
        kernel,
        out_shape=jax.ShapeDtypeStruct((2, QB, SEC), BF16),
        in_specs=[pl.BlockSpec(memory_space=pltpu.HBM)] * 7,
        out_specs=pl.BlockSpec(memory_space=pltpu.VMEM),
        scratch_shapes=[
            vmem((PP, 2, RC), BF16),
            vmem((2, TAPS), BF16),
            vmem((2, PS, QB), BF16),
            vmem((1, PS), jnp.int32),
            vmem((20, 16, QB), BF16),
            vmem((5, 2, QB), jnp.int32),
            vmem((5, 2, QB), jnp.int32),
            vmem((PP, 2, TAPS), BF16),
            vmem((16, RC), F32),
            vmem((48, 16, 2 * CB), BF16),
            vmem((2 * CB, TAPS + 2 * CB), BF16),
            vmem((16, RC), BF16),
            vmem((2, NX, 16, SEC), BF16),
            vmem((NCH, NY, BLK, CW), BF16),
            vmem((20, 16, QB), BF16),
            vmem((4, 8, 16, QB), BF16),
            vmem((4, 8, QB), jnp.int32),
            vmem((15, 2 * QB, 2 * QB), BF16),
            vmem((32, 2 * QB), BF16),
            vmem((2 * PS, 2 * QB), BF16),
            vmem((4 * PS, 2 * QB), BF16),
            vmem((8 * PS, 2 * QB), BF16),
            vmem((368, 2 * QB), BF16),
            vmem((NY * BLK, 2 * QB), BF16),
            vmem((4 * QB, NY * BLK), BF16),
            vmem((NCH, 2, QB, CW), BF16),
            vmem((NCH, 2, QB, CW), F32),
            vmem((NCH, 2, QB, CW), BF16),
            dma((7,)),
            dma, dma,
            dma((2, 4)), dma((2, 4)),
            dma((4,)), dma((4,)),
            dma((2, NX)), dma((2, NX)),
            dma((2, NCH, 4)), dma((2, NCH, 4)),
            dma((NCH,)), dma((NCH,)),
        ],
        compiler_params=pltpu.CompilerParams(
            collective_id=0, has_side_effects=True, vmem_limit_bytes=40 << 20
        ),
        name="aperture",
    )(*(pltpu.with_memory_space_constraint(arg, pltpu.HBM) for arg in args))
    return image[:, :, None, :]


def solution(mesh):
    return jax.shard_map(
        on_device,
        mesh=mesh,
        in_specs=(
            P(None, "sub", "section", "rng"),
            P(),
            P(None, "sub", None, None),
            P("sub", None),
            P(None, "sub", None, None, None, None),
            P(None, "sub", None, None),
            P(None, "sub", None, None),
        ),
        out_specs=P(None, "sub", "rng", "section"),
        check_vma=False,
    )
```

```python
import functools

import jax
import jax.numpy as jnp
from jax import lax
from jax.experimental import pallas as pl
from jax.experimental.pallas import tpu as pltpu
from jax.sharding import PartitionSpec as P

F32 = jnp.float32
BF16 = jnp.bfloat16
MESH = pl.DeviceIdType.MESH

NX = 4
NY = 8
NZ = 4
NG = 4
PP = 6
PS = 24
RC = 4096
TAPS = 2048
CB = 128
QB = 128
SEC = 1024
NCH = 8
CW = SEC // NCH
BLK = 4 * PS


def staggered(chunks, lag):
    steps = [(2 * s + lag * c, c, s) for c in range(chunks) for s in range(5)]
    return [(c, s) for _, c, s in sorted(steps)]


ORDER = staggered(NCH, 0.7)


def dot(a, b):
    return jnp.dot(a, b, preferred_element_type=F32)


def dot_nt(a, b):
    return lax.dot_general(a, b, (((1,), (1,)), ((), ())), preferred_element_type=F32)


def flip(v, bit):
    return v + bit - 2 * bit * ((v // bit) % 2)


def one_hot(shape, dim0_of_dim1):
    rows = lax.broadcasted_iota(jnp.int32, shape, 0)
    cols = lax.broadcasted_iota(jnp.int32, shape, 1)
    return jnp.where(rows == dim0_of_dim1(cols), 1.0, 0.0).astype(BF16)


def kernel(
    echo_h, chirp_h, steer_h, order_h, coef_h, start_h, width_h, out,
    echo, chirp, steer, order, coef, start, width,
    halo, xf, x2, table, comp, recv, gath, pmat, zcoef, zstart, mats,
    tx0, tx1, tx2, tx3, ts, tt, tmat, psend, own, got,
    s_in, s_rim, r_rim, s_par, r_par, s_t, r_t, s_a, r_a, s_g, r_g, s_p, r_p,
):
    loads = []
    pairs = ((steer_h, steer), (order_h, order), (chirp_h, chirp), (coef_h, coef),
             (start_h, start), (width_h, width), (echo_h, echo))
    for i, (src, dst) in enumerate(pairs):
        loads.append(pltpu.make_async_copy(src, dst, s_in.at[i]))
        loads[-1].start()

    sec = lax.axis_index("section")
    sub = lax.axis_index("sub")
    rng = lax.axis_index("rng")
    y = sub % NY
    z = sub // NY
    base = z * NY

    def at_y(v):
        return {"sub": base + v}

    def at_z(v):
        return {"sub": v * NY + y}

    z1 = flip(z, 1)
    z2 = flip(z, 2)
    z3 = flip(z2, 1)
    y1 = flip(y, 1)
    y2 = flip(y, 2)
    y4 = flip(y, 4)
    up = (y + 1) % NY
    down = (y + NY - 1) % NY

    barrier = pltpu.get_barrier_semaphore()
    peers = [{"rng": (rng + 1) % NG}, {"rng": (rng + NG - 1) % NG}]
    for d in range(1, NX):
        other = (sec + d) % NX
        peers.append({"section": other})
        peers.append({"section": other, "sub": z2 * NY + y})
    peers += [at_z(z1), at_z(z2), at_z(z3), at_y(up), at_y(down), at_y(flip(y, 2)), at_y(y4)]
    for peer in peers:
        pl.semaphore_signal(barrier, inc=1, device_id=peer, device_id_type=MESH)
    for i in range(2):
        loads[i].wait()
    select = one_hot((PS, PS), lambda cols: order[...])
    eye32 = one_hot((32, PS), lambda cols: cols)
    sel_t = dot_nt(eye32, select).astype(BF16)
    ts[0:32, 0:QB] = dot(sel_t, steer[0]).astype(BF16)
    ts[0:32, QB:] = dot(sel_t, steer[1]).astype(BF16)

    loads[2].wait()
    wide = TAPS + 2 * CB
    for part in range(2):
        line = jnp.concatenate([chirp[part : part + 1, :].astype(F32), jnp.zeros((1, 2 * CB), F32)], axis=1)
        line = jnp.broadcast_to(line, (CB, wide))
        table[part * CB : (part + 1) * CB, :] = pltpu.roll(line, 0, 1, stride=1, stride_axis=0).astype(BF16)

    def load_rows(ref, blocks, first):
        lanes = blocks * CB
        for part in range(2):
            for p in range(PP):
                xf[part * 8 + p : part * 8 + p + 1, 0:lanes] = ref[p, part : part + 1, :].astype(F32)
            xf[part * 8 + PP : part * 8 + 8, 0:lanes] = jnp.zeros((8 - PP, lanes), F32)
        for b in range(blocks):
            tile = xf[:, b * CB : (b + 1) * CB]
            if ref is halo:
                tile = jnp.where(rng == NG - 1, jnp.zeros_like(tile), tile)
            tile = tile.astype(BF16)
            x2[first + b, :, 0:CB] = tile
            if first + b > 0:
                x2[first + b - 1, :, CB:] = tile

    nb = RC // CB
    nh = TAPS // CB

    def compress(first):
        rows = 16
        total = None
        for j in range(wide // (2 * CB)):
            lhs = x2[first + 2 * j : first + 2 * j + rows].reshape(rows * 16, 2 * CB)
            piece = dot_nt(lhs, table[:, 2 * j * CB : 2 * (j + 1) * CB])
            total = piece if total is None else total + piece
        for b in range(rows):
            re_rows = total[b * 16 : b * 16 + 8]
            im_rows = total[b * 16 + 8 : b * 16 + 16]
            re = re_rows[:, 0:CB] + im_rows[:, CB:]
            im = im_rows[:, 0:CB] - re_rows[:, CB:]
            at = (first + b) * CB
            comp[:, at : at + CB] = jnp.concatenate([re, im], axis=0).astype(BF16)

    loads[6].wait()
    load_rows(echo, nb, 0)
    compress(0)

    pl.semaphore_wait(barrier, len(peers))

    def send(src, dst, ssem, rsem, to):
        return pltpu.make_async_remote_copy(
            src_ref=src, dst_ref=dst, send_sem=ssem, recv_sem=rsem,
            device_id=to, device_id_type=MESH,
        )

    rim = send(echo_h.at[:, :, 0:TAPS], halo, s_rim, r_rim, {"rng": (rng + NG - 1) % NG})

    @pl.when(rng > 0)
    def _():
        rim.start()

    t0 = send(ts.at[0:32], tx0, s_t.at[0], r_t.at[0], at_y(y1))
    t0.start()

    def scatter(s):
        lanes = comp.at[:, s * SEC : (s + 1) * SEC]
        near = send(lanes, recv.at[0, sec], s_a.at[0, s], r_a.at[0, sec], {"section": s})
        far = send(lanes, recv.at[1, sec], s_a.at[1, s], r_a.at[1, sec], {"section": s, "sub": z2 * NY + y})
        far.start()

        @pl.when(sec != s)
        def _():
            near.start()

        return near, far

    sent = [scatter(0), scatter(1)]

    for i in range(3, 6):
        loads[i].wait()
    taps = lax.broadcasted_iota(jnp.int32, (16, QB), 0)
    for level in range(5):
        for side in range(2):
            keep = taps < width[level, side : side + 1, :]
            for part in range(2):
                i = level * 4 + side * 2 + part
                entry = jnp.where(keep, coef[i].astype(F32), 0.0)
                pmat[i] = entry.astype(BF16)
                if level >= 3:
                    zcoef[0, i - 12] = entry.astype(BF16)
            if level >= 3:
                zstart[0, (level - 3) * 2 + side : (level - 3) * 2 + side + 1, :] = start[level, side : side + 1, :]
    zstart[0, 4:8, :] = jnp.zeros((4, QB), jnp.int32)
    par = []
    for d, to, lo, hi in ((1, z1, 2, 8), (2, z2, 0, 2), (3, z3, 2, 4)):
        par.append(send(zcoef.at[0, lo:hi], zcoef.at[d, lo:hi], s_par.at[0, d], r_par.at[0, d], at_z(to)))
        par.append(send(zstart.at[0], zstart.at[d], s_par.at[1, d], r_par.at[1, d], at_z(to)))

    def band(slot, real, imag, first):
        offset = lax.broadcasted_iota(jnp.int32, (QB, QB), 0) - first
        re = jnp.zeros((QB, QB), F32)
        im = jnp.zeros((QB, QB), F32)
        for t in range(16):
            hit = offset == t
            re = jnp.where(hit, real[t : t + 1, :], re)
            im = jnp.where(hit, imag[t : t + 1, :], im)
        re_b = re.astype(BF16)
        mats[slot, 0:QB, 0:QB] = re_b
        mats[slot, QB:, QB:] = re_b
        mats[slot, 0:QB, QB:] = im.astype(BF16)
        mats[slot, QB:, 0:QB] = (-im).astype(BF16)

    def own_band(level, side):
        i = level * 4 + side * 2
        band(level * 2 + side, pmat[i].astype(F32), pmat[i + 1].astype(F32), start[level, side : side + 1, :])

    def far_band(slot, d, row):
        band(slot, zcoef[d, row * 2].astype(F32), zcoef[d, row * 2 + 1].astype(F32), zstart[d, row : row + 1, :])

    def grow(level, mine, theirs, rows):
        at_low = (y // (1 << level)) % 2 == 0
        a = dot(mine, mats[level * 2])[0:rows]
        b = dot(theirs, mats[level * 2 + 1])[0:rows]
        low = jnp.where(at_low, a, b)
        high = jnp.where(at_low, b, a)
        return jnp.concatenate([low, high], axis=0).astype(BF16)

    own_band(0, 0)
    own_band(0, 1)
    t0.wait()
    ts[32:80] = grow(0, ts[0:32], tx0[...], PS)
    t1 = send(ts.at[32:80], tx1, s_t.at[1], r_t.at[1], at_y(y2))
    t1.start()

    @pl.when(rng < NG - 1)
    def _():
        rim.wait_recv()

    load_rows(halo, nh, nb)
    x2[nb + nh - 1, :, CB:] = jnp.zeros((16, CB), BF16)
    compress(16)
    sent += [scatter(2), scatter(3)]
    recv[0, sec] = comp[:, pl.ds(pl.multiple_of(sec * SEC, SEC), SEC)]
    rows_i = lax.broadcasted_iota(jnp.int32, (BLK, 128), 0)
    cols_i = lax.broadcasted_iota(jnp.int32, (BLK, 128), 1)
    hot = jnp.zeros((BLK, 128), F32)
    for zz in range(2):
        for part in range(2):
            for x in range(NX):
                r0 = zz * 2 * PS + part * PS + x * PP
                c0 = zz * 64 + x * 16 + part * 8
                inside = (rows_i >= r0) & (rows_i < r0 + PP) & (cols_i - rows_i == c0 - r0)
                hot = jnp.where(inside, 1.0, hot)
    hot = hot.astype(BF16)
    own_band(1, 0)
    own_band(1, 1)
    t1.wait()
    ts[80:176] = grow(1, ts[32:80], tx1[...], 2 * PS)
    t2 = send(ts.at[80:176], tx2, s_t.at[2], r_t.at[2], at_y(y4))
    t2.start()

    for x in range(NX):
        for zz in range(2):
            arrival = send(comp.at[:, 0:SEC], recv.at[zz, x], s_a.at[zz, 0], r_a.at[zz, x], {"section": sec})
            if zz == 0:
                @pl.when(sec != x)
                def _():
                    arrival.wait_recv()
            else:
                arrival.wait_recv()
    for c in range(NCH):
        rows = recv[:, :, :, c * CW : (c + 1) * CW].reshape(2 * NX * 16, CW)
        gath[c, y] = dot(hot, rows).astype(BF16)

    def hop(direction, c, s):
        if direction == 0:
            at = (y + NY - s) % NY
            to = up
        else:
            at = (y + s) % NY
            to = down
        return send(gath.at[c, at], gath.at[c, at], s_g.at[direction, c, s], r_g.at[direction, c, s], at_y(to))

    def arrived(direction, c, s):
        if direction == 0:
            at = (y + 2 * NY - 1 - s) % NY
        else:
            at = (y + 1 + s) % NY
        return send(gath.at[c, at], gath.at[c, at], s_g.at[direction, c, s], r_g.at[direction, c, s], at_y(up))

    def legs(c, s):
        return (0, 1) if s < 3 else (c % 2,)

    def ring(c, s):
        for direction in legs(c, s):
            if s > 0:
                arrived(direction, c, s - 1).wait_recv()
            hop(direction, c, s).start()

    def settle(c):
        for direction in (0, 1):
            arrived(direction, c, 3 if direction in legs(c, 3) else 2).wait_recv()

    state = {}

    def part_a():
        for copy in par:
            copy.start()
        own_band(2, 0)
        own_band(2, 1)
        t2.wait()
        ts[176:368] = grow(2, ts[80:176], tx2[...], 4 * PS)
        state["t3"] = send(ts.at[176:368], tx3, s_t.at[3], r_t.at[3], at_z(z2))
        state["t3"].start()

    def part_b():
        for level in (3, 4):
            for side in range(2):
                own_band(level, side)

    def part_c():
        for copy in par:
            copy.wait()
        far_band(10, 1, 1)
        far_band(11, 1, 2)
        far_band(12, 1, 3)
        far_band(13, 2, 0)
        far_band(14, 3, 1)

    def chain(rows, first, second):
        return dot(dot(rows, mats[first]).astype(BF16), mats[second]).reshape(NY, PS, 2 * QB)

    def turned(rows):
        return jnp.concatenate([-rows[:, :, QB:], rows[:, :, 0:QB]], axis=2)

    eye = one_hot((2 * QB, 2 * QB), lambda cols: cols)

    def part_d():
        near_rows = ts[176:368]
        a0 = chain(near_rows, 6, 8)
        b0 = chain(near_rows, 10, 11)
        state["t3"].wait()
        far_rows = tx3[...]
        a1 = chain(far_rows, 13, 9)
        b1 = chain(far_rows, 14, 12)
        for i, (near_t, far_t) in enumerate(((a0, a1), (b0, b1))):
            full = jnp.concatenate([near_t, turned(near_t), far_t, turned(far_t)], axis=1)
            tt[...] = full.reshape(NY * BLK, 2 * QB).astype(BF16)
            tmat[i * 2 * QB : (i + 1) * 2 * QB, :] = dot_nt(eye, tt[...]).astype(BF16)

    swaps = []

    def image(c):
        settle(c)
        pulses = gath[c].reshape(NY * BLK, CW)
        psend[c] = dot(tmat[2 * QB :, :], pulses).reshape(2, QB, CW).astype(BF16)
        swap = send(psend.at[c], got.at[c], s_p.at[c], r_p.at[c], at_z(z1))
        swap.start()
        swaps.append(swap)
        own[c] = dot(tmat[0 : 2 * QB, :], pulses).reshape(2, QB, CW)

    parts = {NCH: part_a, NCH + NCH // 2: part_b, 2 * NCH: part_c, 2 * NCH + NCH // 2: part_d}
    for i, (c, s) in enumerate(ORDER):
        if s == 4:
            image(c)
        else:
            ring(c, s)
        if i + 1 in parts:
            parts[i + 1]()
    for (c, _), swap in zip([step for step in ORDER if step[1] == 4], swaps):
        swap.wait()
        out[:, :, c * CW : (c + 1) * CW] = (own[c] + got[c].astype(F32)).astype(BF16)
    for s, (near, far) in enumerate(sent):
        far.wait_send()

        @pl.when(sec != s)
        def _():
            near.wait_send()

    @pl.when(rng > 0)
    def _():
        rim.wait_send()

    for c in range(NCH):
        for s in range(4):
            for direction in legs(c, s):
                hop(direction, c, s).wait_send()


def on_device(echoes, chirp, steer, pulse_order, band_coef, band_start, band_width):
    echo = jnp.transpose(echoes[:, 0], (1, 0, 2))
    steer_t = jnp.swapaxes(steer[:, 0], 1, 2)
    coef = jnp.swapaxes(band_coef[:, 0], 3, 4).reshape(20, 16, QB)
    args = (echo, chirp, steer_t, pulse_order, coef, band_start[:, 0], band_width[:, 0])
    dma = pltpu.SemaphoreType.DMA
    vmem = pltpu.VMEM
    image = pl.pallas_call(
        kernel,
        out_shape=jax.ShapeDtypeStruct((2, QB, SEC), BF16),
        in_specs=[pl.BlockSpec(memory_space=pltpu.HBM)] * 7,
        out_specs=pl.BlockSpec(memory_space=pltpu.VMEM),
        scratch_shapes=[
            vmem((PP, 2, RC), BF16),
            vmem((2, TAPS), BF16),
            vmem((2, PS, QB), BF16),
            vmem((1, PS), jnp.int32),
            vmem((20, 16, QB), BF16),
            vmem((5, 2, QB), jnp.int32),
            vmem((5, 2, QB), jnp.int32),
            vmem((PP, 2, TAPS), BF16),
            vmem((16, RC), F32),
            vmem((48, 16, 2 * CB), BF16),
            vmem((2 * CB, TAPS + 2 * CB), BF16),
            vmem((16, RC), BF16),
            vmem((2, NX, 16, SEC), BF16),
            vmem((NCH, NY, BLK, CW), BF16),
            vmem((20, 16, QB), BF16),
            vmem((4, 8, 16, QB), BF16),
            vmem((4, 8, QB), jnp.int32),
            vmem((15, 2 * QB, 2 * QB), BF16),
            vmem((32, 2 * QB), BF16),
            vmem((2 * PS, 2 * QB), BF16),
            vmem((4 * PS, 2 * QB), BF16),
            vmem((8 * PS, 2 * QB), BF16),
            vmem((368, 2 * QB), BF16),
            vmem((NY * BLK, 2 * QB), BF16),
            vmem((4 * QB, NY * BLK), BF16),
            vmem((NCH, 2, QB, CW), BF16),
            vmem((NCH, 2, QB, CW), F32),
            vmem((NCH, 2, QB, CW), BF16),
            dma((7,)),
            dma, dma,
            dma((2, 4)), dma((2, 4)),
            dma((4,)), dma((4,)),
            dma((2, NX)), dma((2, NX)),
            dma((2, NCH, 4)), dma((2, NCH, 4)),
            dma((NCH,)), dma((NCH,)),
        ],
        compiler_params=pltpu.CompilerParams(
            collective_id=0, has_side_effects=True, vmem_limit_bytes=40 << 20
        ),
        name="aperture",
    )(*(pltpu.with_memory_space_constraint(arg, pltpu.HBM) for arg in args))
    return image[:, :, None, :]


def solution(mesh):
    return jax.shard_map(
        on_device,
        mesh=mesh,
        in_specs=(
            P(None, "sub", "section", "rng"),
            P(),
            P(None, "sub", None, None),
            P("sub", None),
            P(None, "sub", None, None, None, None),
            P(None, "sub", None, None),
            P(None, "sub", None, None),
        ),
        out_specs=P(None, "sub", "rng", "section"),
        check_vma=False,
    )
```

```python
import functools

import jax
import jax.numpy as jnp
from jax import lax
from jax.experimental import pallas as pl
from jax.experimental.pallas import tpu as pltpu
from jax.sharding import PartitionSpec as P

F32 = jnp.float32
BF16 = jnp.bfloat16
MESH = pl.DeviceIdType.MESH

NX = 4
NY = 8
NZ = 4
NG = 4
PP = 6
PS = 24
RC = 4096
TAPS = 2048
CB = 128
QB = 128
SEC = 1024
NCH = 8
CW = SEC // NCH
BLK = 4 * PS


def staggered(chunks, lag):
    steps = [(2 * s + lag * c, c, s) for c in range(chunks) for s in range(5)]
    return [(c, s) for _, c, s in sorted(steps)]


ORDER = staggered(NCH, 0.7)


def dot(a, b):
    return jnp.dot(a, b, preferred_element_type=F32)


def dot_nt(a, b):
    return lax.dot_general(a, b, (((1,), (1,)), ((), ())), preferred_element_type=F32)


def flip(v, bit):
    return v + bit - 2 * bit * ((v // bit) % 2)


def one_hot(shape, dim0_of_dim1):
    rows = lax.broadcasted_iota(jnp.int32, shape, 0)
    cols = lax.broadcasted_iota(jnp.int32, shape, 1)
    return jnp.where(rows == dim0_of_dim1(cols), 1.0, 0.0).astype(BF16)


def kernel(
    echo_h, chirp_h, steer_h, order_h, coef_h, start_h, width_h, out,
    echo, chirp, steer, order, coef, start, width,
    halo, xf, x2, table, comp, recv, gath, pmat, zcoef, zstart, mats,
    tx0, tx1, tx2, tx3, ts, tt, tmat, psend, own, got,
    s_in, s_rim, r_rim, s_par, r_par, s_t, r_t, s_a, r_a, s_g, r_g, s_p, r_p,
):
    loads = []
    pairs = ((steer_h, steer), (order_h, order), (chirp_h, chirp), (coef_h, coef),
             (start_h, start), (width_h, width), (echo_h, echo))
    for i, (src, dst) in enumerate(pairs):
        loads.append(pltpu.make_async_copy(src, dst, s_in.at[i]))
        loads[-1].start()

    sec = lax.axis_index("section")
    sub = lax.axis_index("sub")
    rng = lax.axis_index("rng")
    y = sub % NY
    z = sub // NY
    base = z * NY

    def at_y(v):
        return {"sub": base + v}

    def at_z(v):
        return {"sub": v * NY + y}

    z1 = flip(z, 1)
    z2 = flip(z, 2)
    z3 = flip(z2, 1)
    y1 = flip(y, 1)
    y2 = flip(y, 2)
    y4 = flip(y, 4)
    up = (y + 1) % NY
    down = (y + NY - 1) % NY

    barrier = pltpu.get_barrier_semaphore()
    peers = [{"rng": (rng + 1) % NG}, {"rng": (rng + NG - 1) % NG}]
    for d in range(1, NX):
        other = (sec + d) % NX
        peers.append({"section": other})
        peers.append({"section": other, "sub": z2 * NY + y})
    peers += [at_z(z1), at_z(z2), at_z(z3), at_y(up), at_y(down), at_y(flip(y, 2)), at_y(y4)]
    for peer in peers:
        pl.semaphore_signal(barrier, inc=1, device_id=peer, device_id_type=MESH)
    for i in range(2):
        loads[i].wait()
    select = one_hot((PS, PS), lambda cols: order[...])
    eye32 = one_hot((32, PS), lambda cols: cols)
    sel_t = dot_nt(eye32, select).astype(BF16)
    ts[0:32, 0:QB] = dot(sel_t, steer[0]).astype(BF16)
    ts[0:32, QB:] = dot(sel_t, steer[1]).astype(BF16)

    loads[2].wait()
    wide = TAPS + 2 * CB
    for part in range(2):
        line = jnp.concatenate([chirp[part : part + 1, :].astype(F32), jnp.zeros((1, 2 * CB), F32)], axis=1)
        line = jnp.broadcast_to(line, (CB, wide))
        table[part * CB : (part + 1) * CB, :] = pltpu.roll(line, 0, 1, stride=1, stride_axis=0).astype(BF16)

    def load_rows(ref, blocks, first):
        lanes = blocks * CB
        for part in range(2):
            for p in range(PP):
                xf[part * 8 + p : part * 8 + p + 1, 0:lanes] = ref[p, part : part + 1, :].astype(F32)
            xf[part * 8 + PP : part * 8 + 8, 0:lanes] = jnp.zeros((8 - PP, lanes), F32)
        for b in range(blocks):
            tile = xf[:, b * CB : (b + 1) * CB]
            if ref is halo:
                tile = jnp.where(rng == NG - 1, jnp.zeros_like(tile), tile)
            tile = tile.astype(BF16)
            x2[first + b, :, 0:CB] = tile
            if first + b > 0:
                x2[first + b - 1, :, CB:] = tile

    nb = RC // CB
    nh = TAPS // CB

    def compress(first):
        rows = 16
        total = None
        for j in range(wide // (2 * CB)):
            lhs = x2[first + 2 * j : first + 2 * j + rows].reshape(rows * 16, 2 * CB)
            piece = dot_nt(lhs, table[:, 2 * j * CB : 2 * (j + 1) * CB])
            total = piece if total is None else total + piece
        for b in range(rows):
            re_rows = total[b * 16 : b * 16 + 8]
            im_rows = total[b * 16 + 8 : b * 16 + 16]
            re = re_rows[:, 0:CB] + im_rows[:, CB:]
            im = im_rows[:, 0:CB] - re_rows[:, CB:]
            at = (first + b) * CB
            comp[:, at : at + CB] = jnp.concatenate([re, im], axis=0).astype(BF16)

    loads[6].wait()
    load_rows(echo, nb, 0)
    compress(0)

    pl.semaphore_wait(barrier, len(peers))

    def send(src, dst, ssem, rsem, to):
        return pltpu.make_async_remote_copy(
            src_ref=src, dst_ref=dst, send_sem=ssem, recv_sem=rsem,
            device_id=to, device_id_type=MESH,
        )

    rim = send(echo_h.at[:, :, 0:TAPS], halo, s_rim, r_rim, {"rng": (rng + NG - 1) % NG})

    @pl.when(rng > 0)
    def _():
        rim.start()

    t0 = send(ts.at[0:32], tx0, s_t.at[0], r_t.at[0], at_y(y1))
    t0.start()

    def scatter(s):
        lanes = comp.at[:, s * SEC : (s + 1) * SEC]
        near = send(lanes, recv.at[0, sec], s_a.at[0, s], r_a.at[0, sec], {"section": s})
        far = send(lanes, recv.at[1, sec], s_a.at[1, s], r_a.at[1, sec], {"section": s, "sub": z2 * NY + y})
        far.start()

        @pl.when(sec != s)
        def _():
            near.start()

        return near, far

    sent = [scatter(0), scatter(1)]

    for i in range(3, 6):
        loads[i].wait()
    taps = lax.broadcasted_iota(jnp.int32, (16, QB), 0)
    for level in range(5):
        for side in range(2):
            keep = taps < width[level, side : side + 1, :]
            for part in range(2):
                i = level * 4 + side * 2 + part
                entry = jnp.where(keep, coef[i].astype(F32), 0.0)
                pmat[i] = entry.astype(BF16)
                if level >= 3:
                    zcoef[0, i - 12] = entry.astype(BF16)
            if level >= 3:
                zstart[0, (level - 3) * 2 + side : (level - 3) * 2 + side + 1, :] = start[level, side : side + 1, :]
    zstart[0, 4:8, :] = jnp.zeros((4, QB), jnp.int32)
    par = []
    for d, to, lo, hi in ((1, z1, 2, 8), (2, z2, 0, 2), (3, z3, 2, 4)):
        par.append(send(zcoef.at[0, lo:hi], zcoef.at[d, lo:hi], s_par.at[0, d], r_par.at[0, d], at_z(to)))
        par.append(send(zstart.at[0], zstart.at[d], s_par.at[1, d], r_par.at[1, d], at_z(to)))

    def band(slot, real, imag, first):
        offset = lax.broadcasted_iota(jnp.int32, (QB, QB), 0) - first
        re = jnp.zeros((QB, QB), F32)
        im = jnp.zeros((QB, QB), F32)
        for t in range(16):
            hit = offset == t
            re = jnp.where(hit, real[t : t + 1, :], re)
            im = jnp.where(hit, imag[t : t + 1, :], im)
        re_b = re.astype(BF16)
        mats[slot, 0:QB, 0:QB] = re_b
        mats[slot, QB:, QB:] = re_b
        mats[slot, 0:QB, QB:] = im.astype(BF16)
        mats[slot, QB:, 0:QB] = (-im).astype(BF16)

    def own_band(level, side):
        i = level * 4 + side * 2
        band(level * 2 + side, pmat[i].astype(F32), pmat[i + 1].astype(F32), start[level, side : side + 1, :])

    def far_band(slot, d, row):
        band(slot, zcoef[d, row * 2].astype(F32), zcoef[d, row * 2 + 1].astype(F32), zstart[d, row : row + 1, :])

    def grow(level, mine, theirs, rows):
        at_low = (y // (1 << level)) % 2 == 0
        a = dot(mine, mats[level * 2])[0:rows]
        b = dot(theirs, mats[level * 2 + 1])[0:rows]
        low = jnp.where(at_low, a, b)
        high = jnp.where(at_low, b, a)
        return jnp.concatenate([low, high], axis=0).astype(BF16)

    own_band(0, 0)
    own_band(0, 1)
    t0.wait()
    ts[32:80] = grow(0, ts[0:32], tx0[...], PS)
    t1 = send(ts.at[32:80], tx1, s_t.at[1], r_t.at[1], at_y(y2))
    t1.start()

    @pl.when(rng < NG - 1)
    def _():
        rim.wait_recv()

    load_rows(halo, nh, nb)
    x2[nb + nh - 1, :, CB:] = jnp.zeros((16, CB), BF16)
    compress(16)
    sent += [scatter(2), scatter(3)]
    recv[0, sec] = comp[:, pl.ds(pl.multiple_of(sec * SEC, SEC), SEC)]
    rows_i = lax.broadcasted_iota(jnp.int32, (BLK, 128), 0)
    cols_i = lax.broadcasted_iota(jnp.int32, (BLK, 128), 1)
    hot = jnp.zeros((BLK, 128), F32)
    for zz in range(2):
        for part in range(2):
            for x in range(NX):
                r0 = zz * 2 * PS + part * PS + x * PP
                c0 = zz * 64 + x * 16 + part * 8
                inside = (rows_i >= r0) & (rows_i < r0 + PP) & (cols_i - rows_i == c0 - r0)
                hot = jnp.where(inside, 1.0, hot)
    hot = hot.astype(BF16)
    own_band(1, 0)
    own_band(1, 1)
    t1.wait()
    ts[80:176] = grow(1, ts[32:80], tx1[...], 2 * PS)
    t2 = send(ts.at[80:176], tx2, s_t.at[2], r_t.at[2], at_y(y4))
    t2.start()

    for x in range(NX):
        for zz in range(2):
            arrival = send(comp.at[:, 0:SEC], recv.at[zz, x], s_a.at[zz, 0], r_a.at[zz, x], {"section": sec})
            if zz == 0:
                @pl.when(sec != x)
                def _():
                    arrival.wait_recv()
            else:
                arrival.wait_recv()
    for c in range(NCH):
        rows = recv[:, :, :, c * CW : (c + 1) * CW].reshape(2 * NX * 16, CW)
        gath[c, y] = dot(hot, rows).astype(BF16)

    def hop(direction, c, s):
        if direction == 0:
            at = (y + NY - s) % NY
            to = up
        else:
            at = (y + s) % NY
            to = down
        return send(gath.at[c, at], gath.at[c, at], s_g.at[direction, c, s], r_g.at[direction, c, s], at_y(to))

    def arrived(direction, c, s):
        if direction == 0:
            at = (y + 2 * NY - 1 - s) % NY
        else:
            at = (y + 1 + s) % NY
        return send(gath.at[c, at], gath.at[c, at], s_g.at[direction, c, s], r_g.at[direction, c, s], at_y(up))

    def legs(c, s):
        return (0, 1) if s < 3 else (c % 2,)

    def ring(c, s):
        for direction in legs(c, s)[:: 1 if c % 2 else -1]:
            if s > 0:
                arrived(direction, c, s - 1).wait_recv()
            hop(direction, c, s).start()

    def settle(c):
        for direction in (0, 1):
            arrived(direction, c, 3 if direction in legs(c, 3) else 2).wait_recv()

    state = {}

    def part_a():
        for copy in par:
            copy.start()
        own_band(2, 0)
        own_band(2, 1)
        t2.wait()
        ts[176:368] = grow(2, ts[80:176], tx2[...], 4 * PS)
        state["t3"] = send(ts.at[176:368], tx3, s_t.at[3], r_t.at[3], at_z(z2))
        state["t3"].start()

    def part_b():
        for level in (3, 4):
            for side in range(2):
                own_band(level, side)

    def part_c():
        for copy in par:
            copy.wait()
        far_band(10, 1, 1)
        far_band(11, 1, 2)
        far_band(12, 1, 3)
        far_band(13, 2, 0)
        far_band(14, 3, 1)

    def chain(rows, first, second):
        return dot(dot(rows, mats[first]).astype(BF16), mats[second]).reshape(NY, PS, 2 * QB)

    def turned(rows):
        return jnp.concatenate([-rows[:, :, QB:], rows[:, :, 0:QB]], axis=2)

    eye = one_hot((2 * QB, 2 * QB), lambda cols: cols)

    def part_d():
        near_rows = ts[176:368]
        a0 = chain(near_rows, 6, 8)
        b0 = chain(near_rows, 10, 11)
        state["t3"].wait()
        far_rows = tx3[...]
        a1 = chain(far_rows, 13, 9)
        b1 = chain(far_rows, 14, 12)
        for i, (near_t, far_t) in enumerate(((a0, a1), (b0, b1))):
            full = jnp.concatenate([near_t, turned(near_t), far_t, turned(far_t)], axis=1)
            tt[...] = full.reshape(NY * BLK, 2 * QB).astype(BF16)
            tmat[i * 2 * QB : (i + 1) * 2 * QB, :] = dot_nt(eye, tt[...]).astype(BF16)

    swaps = []

    def image(c):
        settle(c)
        pulses = gath[c].reshape(NY * BLK, CW)
        psend[c] = dot(tmat[2 * QB :, :], pulses).reshape(2, QB, CW).astype(BF16)
        swap = send(psend.at[c], got.at[c], s_p.at[c], r_p.at[c], at_z(z1))
        swap.start()
        swaps.append(swap)
        own[c] = dot(tmat[0 : 2 * QB, :], pulses).reshape(2, QB, CW)

    parts = {NCH: part_a, NCH + NCH // 2: part_b, 2 * NCH: part_c, 2 * NCH + NCH // 2: part_d}
    for i, (c, s) in enumerate(ORDER):
        if s == 4:
            image(c)
        else:
            ring(c, s)
        if i + 1 in parts:
            parts[i + 1]()
    for (c, _), swap in zip([step for step in ORDER if step[1] == 4], swaps):
        swap.wait()
        out[:, :, c * CW : (c + 1) * CW] = (own[c] + got[c].astype(F32)).astype(BF16)
    for s, (near, far) in enumerate(sent):
        far.wait_send()

        @pl.when(sec != s)
        def _():
            near.wait_send()

    @pl.when(rng > 0)
    def _():
        rim.wait_send()

    for c in range(NCH):
        for s in range(4):
            for direction in legs(c, s):
                hop(direction, c, s).wait_send()


def on_device(echoes, chirp, steer, pulse_order, band_coef, band_start, band_width):
    echo = jnp.transpose(echoes[:, 0], (1, 0, 2))
    steer_t = jnp.swapaxes(steer[:, 0], 1, 2)
    coef = jnp.swapaxes(band_coef[:, 0], 3, 4).reshape(20, 16, QB)
    args = (echo, chirp, steer_t, pulse_order, coef, band_start[:, 0], band_width[:, 0])
    dma = pltpu.SemaphoreType.DMA
    vmem = pltpu.VMEM
    image = pl.pallas_call(
        kernel,
        out_shape=jax.ShapeDtypeStruct((2, QB, SEC), BF16),
        in_specs=[pl.BlockSpec(memory_space=pltpu.HBM)] * 7,
        out_specs=pl.BlockSpec(memory_space=pltpu.VMEM),
        scratch_shapes=[
            vmem((PP, 2, RC), BF16),
            vmem((2, TAPS), BF16),
            vmem((2, PS, QB), BF16),
            vmem((1, PS), jnp.int32),
            vmem((20, 16, QB), BF16),
            vmem((5, 2, QB), jnp.int32),
            vmem((5, 2, QB), jnp.int32),
            vmem((PP, 2, TAPS), BF16),
            vmem((16, RC), F32),
            vmem((48, 16, 2 * CB), BF16),
            vmem((2 * CB, TAPS + 2 * CB), BF16),
            vmem((16, RC), BF16),
            vmem((2, NX, 16, SEC), BF16),
            vmem((NCH, NY, BLK, CW), BF16),
            vmem((20, 16, QB), BF16),
            vmem((4, 8, 16, QB), BF16),
            vmem((4, 8, QB), jnp.int32),
            vmem((15, 2 * QB, 2 * QB), BF16),
            vmem((32, 2 * QB), BF16),
            vmem((2 * PS, 2 * QB), BF16),
            vmem((4 * PS, 2 * QB), BF16),
            vmem((8 * PS, 2 * QB), BF16),
            vmem((368, 2 * QB), BF16),
            vmem((NY * BLK, 2 * QB), BF16),
            vmem((4 * QB, NY * BLK), BF16),
            vmem((NCH, 2, QB, CW), BF16),
            vmem((NCH, 2, QB, CW), F32),
            vmem((NCH, 2, QB, CW), BF16),
            dma((7,)),
            dma, dma,
            dma((2, 4)), dma((2, 4)),
            dma((4,)), dma((4,)),
            dma((2, NX)), dma((2, NX)),
            dma((2, NCH, 4)), dma((2, NCH, 4)),
            dma((NCH,)), dma((NCH,)),
        ],
        compiler_params=pltpu.CompilerParams(
            collective_id=0, has_side_effects=True, vmem_limit_bytes=40 << 20
        ),
        name="aperture",
    )(*(pltpu.with_memory_space_constraint(arg, pltpu.HBM) for arg in args))
    return image[:, :, None, :]


def solution(mesh):
    return jax.shard_map(
        on_device,
        mesh=mesh,
        in_specs=(
            P(None, "sub", "section", "rng"),
            P(),
            P(None, "sub", None, None),
            P("sub", None),
            P(None, "sub", None, None, None, None),
            P(None, "sub", None, None),
            P(None, "sub", None, None),
        ),
        out_specs=P(None, "sub", "rng", "section"),
        check_vma=False,
    )
```
